32 devices in a mesh: tm: 8 (over y, x, core), group: 4 (over z).
Axes of the slice: x: 2, y: 2, z: 4, core: 2. Of those that a mesh axis runs over, the one named last changes fastest.
Arguments:
- frames: bfloat16 [4, 65536, 512], P('group', 'tm')
- pair_count: int32 [4], P('group'), may hold values from 32768 to 63488, as said below
Outputs:
- group_instant: float32 [4, 512, 512], P('group', 'tm')
- group_lagged: float32 [4, 512, 512], P('group', 'tm')
- pooled_instant: float32 [512, 512], P('tm')
- pooled_lagged: float32 [512, 512], P('tm')
The draws below stay inside these ranges and needn't reach their ends.
Inputs may be any that keep to these rules, and one draw needn't show every extreme that they name: `pair_count`: every session has between 32768 and 63488 pairs, and some session has exactly 63488.
All inputs are finite; a program needn't handle non-finite values.
Results may differ from the reference program's by a relative error of at most 0.0003.
Values may be sent and summed in bfloat16 or wider, within the bound.
A program may use at most 64 MiB of HBM per device.

```python
import math
import jax
import jax.numpy as jnp
from jax import lax

F = 512
LAG = 2048
FRAMES_SEQ = 65536
GROUPS = 4


def draw_frames(key, part):
    modes = 64
    keys = jax.random.split(key, 5)
    freq = jnp.exp(jax.random.uniform(keys[0], (modes,), jnp.float32, math.log(2.0 * math.pi / (4.0 * LAG)), math.log(2.0 * math.pi / 16.0)))
    phase = jax.random.uniform(keys[1], (GROUPS, modes), jnp.float32, 0.0, 2.0 * math.pi)
    mixing = jax.random.normal(keys[2], (modes, F), jnp.float32) / math.sqrt(128.0)
    offset = 0.5 * jax.random.normal(keys[3], (GROUPS, F), jnp.float32)
    times = jnp.arange(FRAMES_SEQ, dtype=jnp.float32)
    envelope = 1.0 + 2.0 * times / FRAMES_SEQ

    def one_session(index):
        waves = jnp.sin(times[:, None] * freq[None] + phase[index][None])
        signal = jnp.dot(waves, mixing) * envelope[:, None]
        noise = jax.random.normal(jax.random.fold_in(keys[4], index), (FRAMES_SEQ, F), jnp.float32)
        return (signal + noise + offset[index][None]).astype(jnp.bfloat16)
    return lax.map(one_session, jnp.arange(GROUPS, dtype=jnp.int32))


def draw_pair_count(key, part):
    keys = jax.random.split(jax.random.fold_in(key, 17), 2)
    lowest = FRAMES_SEQ // 2
    highest = FRAMES_SEQ - LAG
    values = jax.random.randint(keys[0], (GROUPS,), lowest, highest + 1, jnp.int32)
    which = jax.random.randint(keys[1], (), 0, GROUPS, jnp.int32)
    return jnp.where(jnp.arange(GROUPS, dtype=jnp.int32) == which, highest, values).astype(jnp.int32)


def setup_inputs(seed: int = 0) -> dict:
    arg_keys = jax.random.split(jax.random.key(seed), 3)
    frames = draw_frames(jax.random.fold_in(arg_keys[2], 71), 0)
    pair_count = draw_pair_count(jax.random.fold_in(arg_keys[2], 71), 0)
    return dict(frames=frames, pair_count=pair_count)


def per_group(item):
    block, count = item
    span = FRAMES_SEQ - LAG
    wide = block[:span].astype(jnp.float32)
    later = block[LAG:].astype(jnp.float32)
    weight = (jnp.arange(span, dtype=jnp.int32) < count).astype(jnp.float32)[:, None]
    number = count.astype(jnp.float32)
    sum_x = jnp.sum(wide * weight, axis=0)
    sum_y = jnp.sum(later * weight, axis=0)
    cent_x = (wide - sum_x / number) * weight
    cent_y = (later - sum_y / number) * weight
    inst = jnp.dot(cent_x.T, cent_x, precision=lax.Precision.HIGHEST, preferred_element_type=jnp.float32)
    lagm = jnp.dot(cent_x.T, cent_y, precision=lax.Precision.HIGHEST, preferred_element_type=jnp.float32)
    return inst, lagm, sum_x, sum_y


def reference(frames, pair_count):
    inst, lagm, sum_x, sum_y = lax.map(per_group, (frames, pair_count))
    number = pair_count.astype(jnp.float32)
    group_instant = inst / number[:, None, None]
    group_lagged = lagm / number[:, None, None]
    total = jnp.sum(number)
    mean_x = sum_x / number[:, None]
    mean_y = sum_y / number[:, None]
    glob_x = jnp.sum(sum_x, axis=0) / total
    glob_y = jnp.sum(sum_y, axis=0) / total
    dev_x = mean_x - glob_x[None]
    dev_y = mean_y - glob_y[None]
    spread_i = jnp.einsum("g,gi,gj->ij", number, dev_x, dev_x, precision=lax.Precision.HIGHEST)
    spread_l = jnp.einsum("g,gi,gj->ij", number, dev_x, dev_y, precision=lax.Precision.HIGHEST)
    pooled_instant = (jnp.sum(inst, axis=0) + spread_i) / total
    pooled_lagged = (jnp.sum(lagm, axis=0) + spread_l) / total
    return group_instant, group_lagged, pooled_instant, pooled_lagged
```

```python
import functools

import jax
import jax.numpy as jnp
from jax import lax
from jax.experimental import pallas as pl
from jax.experimental.pallas import tpu as pltpu
from jax.sharding import PartitionSpec as P

LAG = 2048
MESH = pl.DeviceIdType.MESH
PAD = 16
EXTRA = 8


def kernel(
    T, G, count_ref, frames_ref, gi_ref, gl_ref, pi_ref, po_ref,
    x, xt, head, tail, acc, sx, ai, al, r1i, r1l, r2i, r2l, zi, zl, zri, zrl,
    ld, hs, hr, s1, e1, s2, e2, sz, ez,
):
    F = frames_ref.shape[2]
    R = frames_ref.shape[1]
    H = LAG // 2
    NB = R // H
    S = F // T
    Q = T // 2
    steps = G.bit_length() - 1
    me = lax.axis_index("tm")
    z = lax.axis_index("group")
    c = lax.rem(me, 2)
    q = lax.div(me, 2)
    partner = me + 1 - 2 * c
    count = count_ref[0]

    def remote(src, dst, a, b, dev):
        return pltpu.make_async_remote_copy(
            src_ref=src, dst_ref=dst, send_sem=a, recv_sem=b,
            device_id=dev, device_id_type=MESH,
        )

    def load(i):
        return pltpu.make_async_copy(frames_ref.at[0, pl.ds(i * H, H)], x.at[i], ld.at[i])

    for i in range(NB):
        load(i).start()

    zpeer = []
    for k in range(steps):
        bit = lax.rem(lax.div(z, 2**k), 2)
        zpeer.append(z + 2**k * (1 - 2 * bit))
    barrier = pltpu.get_barrier_semaphore()
    for k in range(1, T):
        pl.semaphore_signal(
            barrier, inc=1, device_id={"tm": lax.rem(me + k, T)}, device_id_type=MESH
        )
    for k in range(steps):
        pl.semaphore_signal(barrier, inc=1, device_id={"group": zpeer[k]}, device_id_type=MESH)
    pl.semaphore_wait(barrier, T - 1 + steps)

    def send_head():
        return remote(frames_ref.at[0, pl.ds(0, H)], head, hs.at[0], hr.at[0], {"tm": me - 1})

    def send_tail():
        return remote(frames_ref.at[0, pl.ds(R - H, H)], tail, hs.at[1], hr.at[1], {"tm": me + 1})

    @pl.when(me > 0)
    def _():
        send_head().start()

    @pl.when(me < T - 1)
    def _():
        send_tail().start()

    def put_transposed(block, base, slot):
        rows = lax.broadcasted_iota(jnp.int32, (H, 128), 0) + base
        keep = jnp.where(rows < count, 1.0, 0.0).astype(jnp.bfloat16)
        masked = block * jnp.concatenate([keep] * (F // 128), axis=1)
        xt[slot, 0:F, :] = masked.T
        cols = lax.broadcasted_iota(jnp.int32, (PAD, H), 1) + base
        xt[slot, F:, :] = jnp.where(cols < count, 1.0, 0.0).astype(jnp.bfloat16)

    def product(slot, block):
        return jnp.dot(xt[slot], block, preferred_element_type=jnp.float32)

    acc[...] = jnp.zeros_like(acc)

    def inst_step(i, carry):
        load(i).wait()
        put_transposed(x[i], me * R + i * H, i)
        acc[...] += product(i, x[i])
        return carry

    lax.fori_loop(0, NB, inst_step, 0)
    for d in range(T):
        ai[d % 2, d // 2] = acc[d * S:(d + 1) * S, :]
    sx[...] = acc[F:F + EXTRA, :]
    p1i = remote(ai.at[1 - c], r1i, s1.at[0], e1.at[0], {"tm": partner})
    p1i.start()

    acc[...] = jnp.zeros_like(acc)

    def lag_step(i, carry):
        acc[...] += product(i, x[i + LAG // H])
        return carry

    lax.fori_loop(0, NB - LAG // H, lag_step, 0)

    def spread(buf, landed, row):
        out = []
        for k in range(1, Q):
            q2 = lax.rem(q + k, Q)
            out.append(remote(
                buf.at[c, q2], landed.at[k - 1], s2.at[row, k - 1], e2.at[row, k - 1],
                {"tm": 2 * q2 + c},
            ))
        return out

    p1i.wait_recv()
    for k in range(Q):
        ai[c, k] += r1i[k]
    p2i = spread(ai, r2i, 0)
    for copy in p2i:
        copy.start()

    @pl.when(me < T - 1)
    def _():
        send_head().wait_recv()
        acc[...] += product(NB - 2, head[...])

    @pl.when(me > 0)
    def _():
        send_tail().wait_recv()
        put_transposed(tail[...], me * R - H, NB - 1)
        acc[...] += product(NB - 1, x[1])

    which = lax.broadcasted_iota(jnp.int32, (EXTRA, F), 0)
    sums = jnp.where(which < 3, sx[...], acc[F:F + EXTRA, :])
    for d in range(T):
        al[d % 2, d // 2, 0:S, :] = acc[d * S:(d + 1) * S, :]
        al[d % 2, d // 2, S:, :] = sums
    p1l = remote(al.at[1 - c], r1l, s1.at[1], e1.at[1], {"tm": partner})
    p1l.start()

    def exchange(buf, landed, k, row):
        return remote(
            buf.at[k], landed.at[k], sz.at[row, k], ez.at[row, k], {"group": zpeer[k]}
        )

    for copy in p2i:
        copy.wait_recv()
    total = ai[c, q]
    for k in range(Q - 1):
        total = total + r2i[k]
    zi[0] = total
    zi_copies = [exchange(zi, zri, k, 0) for k in range(steps)]
    zl_copies = [exchange(zl, zrl, k, 1) for k in range(steps)]
    zi_copies[0].start()

    p1l.wait_recv()
    for k in range(Q):
        al[c, k] += r1l[k]
    p2l = spread(al, r2l, 1)
    for copy in p2l:
        copy.start()

    def advance(copies, buf, landed, k):
        copies[k].wait_recv()
        buf[k + 1] = buf[k] + landed[k]
        if k + 1 < steps:
            copies[k + 1].start()

    for k in range(steps - 1):
        advance(zi_copies, zi, zri, k)

    for copy in p2l:
        copy.wait_recv()
    total = al[c, q]
    for k in range(Q - 1):
        total = total + r2l[k]
    number = count.astype(jnp.float32)
    zl[0, 0:S, :] = total[0:S]
    zl[0, S:, :] = jnp.where(which < 6, total[S:], number)
    zl_copies[0].start()

    rows = lax.broadcasted_iota(jnp.int32, (S, F), 0) + me * S
    cols = lax.broadcasted_iota(jnp.int32, (S, F), 1)

    def centred(inst, lagged, extra, out_i, out_l):
        n = extra[6:7, :]
        mx = extra[0:1, :] / n
        my = extra[3:4, :] / n
        column = jnp.sum(jnp.where(rows == cols, jnp.broadcast_to(mx, (S, F)), 0.0), axis=1, keepdims=True)
        out_i(inst / n - column * mx)
        out_l(lagged / n - column * my)

    def put(ref, lead):
        def store(v):
            if lead:
                ref[0] = v
            else:
                ref[...] = v
        return store

    centred(zi[0], zl[0, 0:S, :], zl[0, S:, :], put(gi_ref, True), put(gl_ref, True))
    advance(zi_copies, zi, zri, steps - 1)
    for k in range(steps):
        advance(zl_copies, zl, zrl, k)
    centred(
        zi[steps], zl[steps, 0:S, :], zl[steps, S:, :], put(pi_ref, False), put(po_ref, False)
    )

    @pl.when(me > 0)
    def _():
        send_head().wait_send()

    @pl.when(me < T - 1)
    def _():
        send_tail().wait_send()

    for copy in [p1i, p1l, *p2i, *p2l, *zi_copies, *zl_copies]:
        copy.wait_send()


def on_device(T, G, frames, pair_count):
    _, R, F = frames.shape
    S, Q, H = F // T, T // 2, LAG // 2
    NB = R // H
    steps = G.bit_length() - 1
    f32, bf16 = jnp.float32, jnp.bfloat16
    V, D = pltpu.VMEM, pltpu.SemaphoreType.DMA
    vmem = pl.BlockSpec(memory_space=pltpu.VMEM)
    return pl.pallas_call(
        functools.partial(kernel, T, G),
        out_shape=(
            jax.ShapeDtypeStruct((1, S, F), f32),
            jax.ShapeDtypeStruct((1, S, F), f32),
            jax.ShapeDtypeStruct((S, F), f32),
            jax.ShapeDtypeStruct((S, F), f32),
        ),
        in_specs=[pl.BlockSpec(memory_space=pltpu.SMEM), pl.BlockSpec(memory_space=pl.ANY)],
        out_specs=(vmem,) * 4,
        scratch_shapes=[
            V((NB, H, F), bf16),
            V((NB, F + PAD, H), bf16),
            V((H, F), bf16),
            V((H, F), bf16),
            V((F + PAD, F), f32),
            V((EXTRA, F), f32),
            V((2, Q, S, F), f32),
            V((2, Q, S + EXTRA, F), f32),
            V((Q, S, F), f32),
            V((Q, S + EXTRA, F), f32),
            V((Q - 1, S, F), f32),
            V((Q - 1, S + EXTRA, F), f32),
            V((steps + 1, S, F), f32),
            V((steps + 1, S + EXTRA, F), f32),
            V((steps, S, F), f32),
            V((steps, S + EXTRA, F), f32),
            D((NB,)),
            D((2,)),
            D((2,)),
            D((2,)),
            D((2,)),
            D((2, Q - 1)),
            D((2, Q - 1)),
            D((2, steps)),
            D((2, steps)),
        ],
        compiler_params=pltpu.CompilerParams(
            collective_id=0, has_side_effects=True, vmem_limit_bytes=60 * 1024 * 1024
        ),
    )(pair_count, frames)


def solution(mesh):
    in_specs = (P("group", "tm", None), P("group"))
    out_specs = (P("group", "tm", None), P("group", "tm", None), P("tm", None), P("tm", None))
    body = functools.partial(on_device, mesh.shape["tm"], mesh.shape["group"])
    return jax.shard_map(
        body, mesh=mesh, in_specs=in_specs, out_specs=out_specs, check_vma=False
    )
```

```python
import functools

import jax
import jax.numpy as jnp
from jax import lax
from jax.experimental import pallas as pl
from jax.experimental.pallas import tpu as pltpu
from jax.sharding import PartitionSpec as P

LAG = 2048
MESH = pl.DeviceIdType.MESH
PAD = 16
EXTRA = 8
CUTS = 4
HALVES = 2


def kernel(
    T, G, count_ref, frames_ref, gi_ref, gl_ref, pi_ref, po_ref,
    x, xt, head, tail, acc, sx, ai, al, r1i, r1l, r2i, r2l, zi, zl, zri, zrl,
    ld, hs, hr, s1, e1, s2, e2, sz, ez,
):
    F = frames_ref.shape[2]
    R = frames_ref.shape[1]
    H = LAG // CUTS
    NB = R // H
    W = F // HALVES
    S = F // T
    Q = T // 2
    steps = G.bit_length() - 1
    me = lax.axis_index("tm")
    z = lax.axis_index("group")
    c = lax.rem(me, 2)
    q = lax.div(me, 2)
    partner = me + 1 - 2 * c
    count = count_ref[0]

    def remote(src, dst, a, b, dev):
        return pltpu.make_async_remote_copy(
            src_ref=src, dst_ref=dst, send_sem=a, recv_sem=b,
            device_id=dev, device_id_type=MESH,
        )

    def load(i):
        return pltpu.make_async_copy(frames_ref.at[0, pl.ds(i * H, H)], x.at[i], ld.at[i])

    for i in range(NB):
        load(i).start()

    zpeer = []
    for k in range(steps):
        bit = lax.rem(lax.div(z, 2**k), 2)
        zpeer.append(z + 2**k * (1 - 2 * bit))
    barrier = pltpu.get_barrier_semaphore()
    for k in range(1, T):
        pl.semaphore_signal(
            barrier, inc=1, device_id={"tm": lax.rem(me + k, T)}, device_id_type=MESH
        )
    for k in range(steps):
        pl.semaphore_signal(barrier, inc=1, device_id={"group": zpeer[k]}, device_id_type=MESH)
    pl.semaphore_wait(barrier, T - 1 + steps)

    def kept(b):
        if T != 8:
            return CUTS // 2
        turn = lax.rem(b, 2) * (1 - lax.rem(lax.div(b, 2), 2))
        return CUTS // 2 + turn * (2 * lax.div(b, 4) - 1)

    before = lax.rem(me + T - 1, T)

    def send_head(j):
        return remote(
            frames_ref.at[0, pl.ds(j * H, H)], head.at[j], hs.at[0, j], hr.at[0, j], {"tm": me - 1}
        )

    def send_tail(j):
        return remote(
            frames_ref.at[0, pl.ds(R - LAG + j * H, H)], tail.at[j], hs.at[1, j], hr.at[1, j],
            {"tm": me + 1},
        )

    def sent(act):
        for j in range(CUTS):
            @pl.when((me > 0) & (j < kept(before)))
            def _():
                act(send_head(j))

            @pl.when((me < T - 1) & (j >= kept(me)))
            def _():
                act(send_tail(j))

    sent(lambda copy: copy.start())

    def put_transposed(block, base, slot):
        rows = lax.broadcasted_iota(jnp.int32, (H, 128), 0) + base
        keep = jnp.where(rows < count, 1.0, 0.0).astype(jnp.bfloat16)
        masked = block * jnp.concatenate([keep] * (F // 128), axis=1)
        xt[slot, 0:F, :] = masked.T
        cols = lax.broadcasted_iota(jnp.int32, (PAD, H), 1) + base
        xt[slot, F:, :] = jnp.where(cols < count, 1.0, 0.0).astype(jnp.bfloat16)

    def product(slot, block):
        return jnp.dot(xt[slot], block, preferred_element_type=jnp.float32)

    acc[...] = jnp.zeros_like(acc)

    def inst_step(i, carry):
        for j in (2 * i, 2 * i + 1):
            load(j).wait()
            put_transposed(x[j], me * R + j * H, j)
        acc[...] += product(2 * i, x[2 * i]) + product(2 * i + 1, x[2 * i + 1])
        return carry

    lax.fori_loop(0, NB // 2, inst_step, 0)
    for d in range(T):
        ai[d % 2, d // 2] = acc[d * S:(d + 1) * S, :]
    sx[...] = acc[F:F + EXTRA, :]
    p1i = remote(ai.at[1 - c], r1i, s1.at[0], e1.at[0], {"tm": partner})
    p1i.start()

    acc[...] = jnp.zeros_like(acc)

    def lag_step(i, carry):
        j = 2 * i
        acc[...] += product(j, x[j + CUTS]) + product(j + 1, x[j + 1 + CUTS])
        return carry

    lax.fori_loop(0, (NB - CUTS) // 2, lag_step, 0)

    def spread(buf, landed, row):
        out = []
        for k in range(1, Q):
            q2 = lax.rem(q + k, Q)
            out.append(remote(
                buf.at[c, q2], landed.at[k - 1], s2.at[row, k - 1], e2.at[row, k - 1],
                {"tm": 2 * q2 + c},
            ))
        return out

    p1i.wait_recv()
    for k in range(Q):
        ai[c, k] += r1i[k]
    p2i = spread(ai, r2i, 0)
    for j in range(CUTS):
        @pl.when((me < T - 1) & (j < kept(me)))
        def _():
            send_head(j).wait_recv()

        @pl.when((me > 0) & (j >= kept(before)))
        def _():
            send_tail(j).wait_recv()
    for copy in p2i:
        copy.start()

    @pl.when(me > 0)
    def _():
        def turn_step(j, carry):
            put_transposed(tail[j], me * R - LAG + j * H, j)
            return carry

        lax.fori_loop(kept(before), CUTS, turn_step, 0)

    which = lax.broadcasted_iota(jnp.int32, (EXTRA, W), 0)
    p1l = []
    for h in range(HALVES):
        cols = slice(h * W, (h + 1) * W)

        @pl.when(me < T - 1)
        def _():
            def head_step(j, carry):
                acc[:, cols] += product(NB - CUTS + j, head[j, :, cols])
                return carry

            lax.fori_loop(0, kept(me), head_step, 0)

        @pl.when(me > 0)
        def _():
            def tail_step(j, carry):
                acc[:, cols] += product(j, x[j, :, cols])
                return carry

            lax.fori_loop(kept(before), CUTS, tail_step, 0)

        sums = jnp.where(which < 3, sx[:, cols], acc[F:F + EXTRA, cols])
        for d in range(T):
            al[h, d % 2, d // 2, 0:S, :] = acc[d * S:(d + 1) * S, cols]
            al[h, d % 2, d // 2, S:, :] = sums
        p1l.append(remote(al.at[h, 1 - c], r1l.at[h], s1.at[1 + h], e1.at[1 + h], {"tm": partner}))
        p1l[h].start()

    def exchange(buf, landed, k, row):
        return remote(
            buf.at[k], landed.at[k], sz.at[row, k], ez.at[row, k], {"group": zpeer[k]}
        )

    p2l = []
    for h in range(HALVES):
        p1l[h].wait_recv()
        for k in range(Q):
            al[h, c, k] += r1l[h, k]
        p2l.append(spread(al.at[h], r2l.at[h], 1 + h))
        for copy in p2l[h]:
            copy.start()

    for copy in p2i:
        copy.wait_recv()
    total = ai[c, q]
    for k in range(Q - 1):
        total = total + r2i[k]
    zi[0] = total
    zi_copies = [exchange(zi, zri, k, 0) for k in range(steps)]
    zl_copies = [
        [exchange(zl.at[h], zrl.at[h], k, 1 + h) for k in range(steps)] for h in range(HALVES)
    ]
    zi_copies[0].start()

    def advance(copies, buf, landed, k):
        copies[k].wait_recv()
        buf[k + 1] = buf[k] + landed[k]
        if k + 1 < steps:
            copies[k + 1].start()

    for k in range(steps - 1):
        advance(zi_copies, zi, zri, k)

    number = count.astype(jnp.float32)
    for h in range(HALVES):
        for copy in p2l[h]:
            copy.wait_recv()
        total = al[h, c, q]
        for k in range(Q - 1):
            total = total + r2l[h, k]
        zl[h, 0, 0:S, :] = total[0:S]
        zl[h, 0, S:, :] = jnp.where(which < 6, total[S:], number)
        zl_copies[h][0].start()

    def lagged(k):
        return jnp.concatenate([zl[h, k] for h in range(HALVES)], axis=1)

    rows = lax.broadcasted_iota(jnp.int32, (S, F), 0) + me * S
    cols = lax.broadcasted_iota(jnp.int32, (S, F), 1)

    def centred(inst, both, out_i, out_l):
        extra = both[S:]
        n = extra[6:7, :]
        mx = extra[0:1, :] / n
        my = extra[3:4, :] / n
        wide = jnp.where(rows == cols, jnp.broadcast_to(mx, (S, F)), 0.0)
        column = jnp.sum(wide, axis=1, keepdims=True)
        out_i(inst / n - column * mx)
        out_l(both[0:S] / n - column * my)

    def put(ref, lead):
        def store(v):
            if lead:
                ref[0] = v
            else:
                ref[...] = v
        return store

    centred(zi[0], lagged(0), put(gi_ref, True), put(gl_ref, True))
    advance(zi_copies, zi, zri, steps - 1)
    for k in range(steps):
        for h in range(HALVES):
            advance(zl_copies[h], zl.at[h], zrl.at[h], k)
    centred(zi[steps], lagged(steps), put(pi_ref, False), put(po_ref, False))

    sent(lambda copy: copy.wait_send())
    for group in [[p1i], p1l, p2i, *p2l, zi_copies, *zl_copies]:
        for copy in group:
            copy.wait_send()


def on_device(T, G, frames, pair_count):
    _, R, F = frames.shape
    S, Q, H, W = F // T, T // 2, LAG // CUTS, F // HALVES
    NB = R // H
    steps = G.bit_length() - 1
    f32, bf16 = jnp.float32, jnp.bfloat16
    V, D = pltpu.VMEM, pltpu.SemaphoreType.DMA
    vmem = pl.BlockSpec(memory_space=pltpu.VMEM)
    return pl.pallas_call(
        functools.partial(kernel, T, G),
        out_shape=(
            jax.ShapeDtypeStruct((1, S, F), f32),
            jax.ShapeDtypeStruct((1, S, F), f32),
            jax.ShapeDtypeStruct((S, F), f32),
            jax.ShapeDtypeStruct((S, F), f32),
        ),
        in_specs=[pl.BlockSpec(memory_space=pltpu.SMEM), pl.BlockSpec(memory_space=pl.ANY)],
        out_specs=(vmem,) * 4,
        scratch_shapes=[
            V((NB, H, F), bf16),
            V((NB, F + PAD, H), bf16),
            V((CUTS, H, F), bf16),
            V((CUTS, H, F), bf16),
            V((F + PAD, F), f32),
            V((EXTRA, F), f32),
            V((2, Q, S, F), f32),
            V((HALVES, 2, Q, S + EXTRA, W), f32),
            V((Q, S, F), f32),
            V((HALVES, Q, S + EXTRA, W), f32),
            V((Q - 1, S, F), f32),
            V((HALVES, Q - 1, S + EXTRA, W), f32),
            V((steps + 1, S, F), f32),
            V((HALVES, steps + 1, S + EXTRA, W), f32),
            V((steps, S, F), f32),
            V((HALVES, steps, S + EXTRA, W), f32),
            D((NB,)),
            D((2, CUTS)),
            D((2, CUTS)),
            D((1 + HALVES,)),
            D((1 + HALVES,)),
            D((1 + HALVES, Q - 1)),
            D((1 + HALVES, Q - 1)),
            D((1 + HALVES, steps)),
            D((1 + HALVES, steps)),
        ],
        compiler_params=pltpu.CompilerParams(
            collective_id=0, has_side_effects=True, vmem_limit_bytes=60 * 1024 * 1024
        ),
    )(pair_count, frames)


def solution(mesh):
    in_specs = (P("group", "tm", None), P("group"))
    out_specs = (P("group", "tm", None), P("group", "tm", None), P("tm", None), P("tm", None))
    body = functools.partial(on_device, mesh.shape["tm"], mesh.shape["group"])
    return jax.shard_map(
        body, mesh=mesh, in_specs=in_specs, out_specs=out_specs, check_vma=False
    )
```

```python
import functools

import jax
import jax.numpy as jnp
from jax import lax
from jax.experimental import pallas as pl
from jax.experimental.pallas import tpu as pltpu
from jax.sharding import PartitionSpec as P

LAG = 2048
MESH = pl.DeviceIdType.MESH
PAD = 16
EXTRA = 8
CUTS = 4
HALVES = 2


def kernel(
    T, G, count_ref, frames_ref, own_ref, all_ref,
    x, xt, head, tail, acc, sx, ai, al, r1i, r1l, r2i, r2l, zi, zl, zri, zrl,
    ld, hs, hr, s1, e1, s2, e2, sz, ez,
):
    F = frames_ref.shape[2]
    R = frames_ref.shape[1]
    H = LAG // CUTS
    NB = R // H
    W = F // HALVES
    S = F // T
    Q = T // 2
    steps = G.bit_length() - 1
    me = lax.axis_index("tm")
    z = lax.axis_index("group")
    c = lax.rem(me, 2)
    q = lax.div(me, 2)
    partner = me + 1 - 2 * c
    count = count_ref[0]

    def remote(src, dst, a, b, dev):
        return pltpu.make_async_remote_copy(
            src_ref=src, dst_ref=dst, send_sem=a, recv_sem=b,
            device_id=dev, device_id_type=MESH,
        )

    def load(i):
        return pltpu.make_async_copy(frames_ref.at[0, pl.ds(i * H, H)], x.at[i], ld.at[i])

    for i in range(NB):
        load(i).start()

    zpeer = []
    for k in range(steps):
        bit = lax.rem(lax.div(z, 2**k), 2)
        zpeer.append(z + 2**k * (1 - 2 * bit))
    barrier = pltpu.get_barrier_semaphore()
    for k in range(1, T):
        pl.semaphore_signal(
            barrier, inc=1, device_id={"tm": lax.rem(me + k, T)}, device_id_type=MESH
        )
    for k in range(steps):
        pl.semaphore_signal(barrier, inc=1, device_id={"group": zpeer[k]}, device_id_type=MESH)
    pl.semaphore_wait(barrier, T - 1 + steps)

    def kept(b):
        if T != 8:
            return CUTS // 2
        turn = lax.rem(b, 2) * (1 - lax.rem(lax.div(b, 2), 2))
        return CUTS // 2 + turn * (2 * lax.div(b, 4) - 1)

    before = lax.rem(me + T - 1, T)

    def send_head(j):
        return remote(
            frames_ref.at[0, pl.ds(j * H, H)], head.at[j], hs.at[0, j], hr.at[0, j], {"tm": me - 1}
        )

    def send_tail(j):
        return remote(
            frames_ref.at[0, pl.ds(R - LAG + j * H, H)], tail.at[j], hs.at[1, j], hr.at[1, j],
            {"tm": me + 1},
        )

    def sent(act):
        for j in range(CUTS):
            @pl.when((me > 0) & (j < kept(before)))
            def _():
                act(send_head(j))

            @pl.when((me < T - 1) & (j >= kept(me)))
            def _():
                act(send_tail(j))

    sent(lambda copy: copy.start())

    def put_transposed(block, base, slot):
        rows = lax.broadcasted_iota(jnp.int32, (H, 128), 0) + base
        keep = jnp.where(rows < count, 1.0, 0.0).astype(jnp.bfloat16)
        masked = block * jnp.concatenate([keep] * (F // 128), axis=1)
        xt[slot, 0:F, :] = masked.T
        cols = lax.broadcasted_iota(jnp.int32, (PAD, H), 1) + base
        xt[slot, F:, :] = jnp.where(cols < count, 1.0, 0.0).astype(jnp.bfloat16)

    def product(slot, block):
        return jnp.dot(xt[slot], block, preferred_element_type=jnp.float32)

    acc[...] = jnp.zeros_like(acc)

    def inst_step(i, carry):
        for j in (2 * i, 2 * i + 1):
            load(j).wait()
            put_transposed(x[j], me * R + j * H, j)
        acc[...] += product(2 * i, x[2 * i]) + product(2 * i + 1, x[2 * i + 1])
        return carry

    lax.fori_loop(0, NB // 2, inst_step, 0)
    for d in range(T):
        ai[d % 2, d // 2] = acc[d * S:(d + 1) * S, :]
    sx[...] = acc[F:F + EXTRA, :]
    p1i = remote(ai.at[1 - c], r1i, s1.at[0], e1.at[0], {"tm": partner})
    p1i.start()

    acc[...] = jnp.zeros_like(acc)

    def lag_step(i, carry):
        j = 2 * i
        acc[...] += product(j, x[j + CUTS]) + product(j + 1, x[j + 1 + CUTS])
        return carry

    lax.fori_loop(0, (NB - CUTS) // 2, lag_step, 0)

    def spread(buf, landed, row):
        out = []
        for k in range(1, Q):
            q2 = lax.rem(q + k, Q)
            out.append(remote(
                buf.at[c, q2], landed.at[k - 1], s2.at[row, k - 1], e2.at[row, k - 1],
                {"tm": 2 * q2 + c},
            ))
        return out

    p1i.wait_recv()
    for k in range(Q):
        ai[c, k] += r1i[k]
    p2i = spread(ai, r2i, 0)
    for j in range(CUTS):
        @pl.when((me < T - 1) & (j < kept(me)))
        def _():
            send_head(j).wait_recv()

        @pl.when((me > 0) & (j >= kept(before)))
        def _():
            send_tail(j).wait_recv()
    for copy in p2i:
        copy.start()

    @pl.when(me > 0)
    def _():
        def turn_step(j, carry):
            put_transposed(tail[j], me * R - LAG + j * H, j)
            return carry

        lax.fori_loop(kept(before), CUTS, turn_step, 0)

    which = lax.broadcasted_iota(jnp.int32, (EXTRA, W), 0)
    p1l = []
    for h in range(HALVES):
        cols = slice(h * W, (h + 1) * W)

        @pl.when(me < T - 1)
        def _():
            def head_step(j, carry):
                acc[:, cols] += product(NB - CUTS + j, head[j, :, cols])
                return carry

            lax.fori_loop(0, kept(me), head_step, 0)

        @pl.when(me > 0)
        def _():
            def tail_step(j, carry):
                acc[:, cols] += product(j, x[j, :, cols])
                return carry

            lax.fori_loop(kept(before), CUTS, tail_step, 0)

        sums = jnp.where(which < 3, sx[:, cols], acc[F:F + EXTRA, cols])
        for d in range(T):
            al[h, d % 2, d // 2, 0:S, :] = acc[d * S:(d + 1) * S, cols]
            al[h, d % 2, d // 2, S:, :] = sums
        p1l.append(remote(al.at[h, 1 - c], r1l.at[h], s1.at[1 + h], e1.at[1 + h], {"tm": partner}))
        p1l[h].start()

    def exchange(buf, landed, k, row):
        return remote(
            buf.at[k], landed.at[k], sz.at[row, k], ez.at[row, k], {"group": zpeer[k]}
        )

    p2l = []
    for h in range(HALVES):
        p1l[h].wait_recv()
        for k in range(Q):
            al[h, c, k] += r1l[h, k]
        p2l.append(spread(al.at[h], r2l.at[h], 1 + h))
        for copy in p2l[h]:
            copy.start()

    for copy in p2i:
        copy.wait_recv()
    total = ai[c, q]
    for k in range(Q - 1):
        total = total + r2i[k]
    zi[0] = total
    zi_copies = [exchange(zi, zri, k, 0) for k in range(steps)]
    zl_copies = [
        [exchange(zl.at[h], zrl.at[h], k, 1 + h) for k in range(steps)] for h in range(HALVES)
    ]
    zi_copies[0].start()

    def advance(copies, buf, landed, k):
        copies[k].wait_recv()
        buf[k + 1] = buf[k] + landed[k]
        if k + 1 < steps:
            copies[k + 1].start()

    for k in range(steps - 1):
        advance(zi_copies, zi, zri, k)

    number = count.astype(jnp.float32)
    for h in range(HALVES):
        for copy in p2l[h]:
            copy.wait_recv()
        total = al[h, c, q]
        for k in range(Q - 1):
            total = total + r2l[h, k]
        zl[h, 0, 0:S, :] = total[0:S]
        zl[h, 0, S:, :] = jnp.where(which < 6, total[S:], number)
        zl_copies[h][0].start()

    def out(ref, k):
        ref[0:S, :] = zi[k]
        for h in range(HALVES):
            ref[S:, h * W:(h + 1) * W] = zl[h, k]

    out(own_ref, 0)
    advance(zi_copies, zi, zri, steps - 1)
    for k in range(steps):
        for h in range(HALVES):
            advance(zl_copies[h], zl.at[h], zrl.at[h], k)
    out(all_ref, steps)

    sent(lambda copy: copy.wait_send())
    for group in [[p1i], p1l, p2i, *p2l, zi_copies, *zl_copies]:
        for copy in group:
            copy.wait_send()


def centre(own_ref, all_ref, gi_ref, gl_ref, pi_ref, po_ref):
    S, F = pi_ref.shape
    rows = lax.broadcasted_iota(jnp.int32, (S, F), 0) + lax.axis_index("tm") * S
    cols = lax.broadcasted_iota(jnp.int32, (S, F), 1)
    for ref, out_i, out_l in ((own_ref, gi_ref.at[0], gl_ref.at[0]), (all_ref, pi_ref, po_ref)):
        n = ref[2 * S + 6:2 * S + 7, :]
        mx = ref[2 * S:2 * S + 1, :] / n
        my = ref[2 * S + 3:2 * S + 4, :] / n
        wide = jnp.where(rows == cols, jnp.broadcast_to(mx, (S, F)), 0.0)
        column = jnp.sum(wide, axis=1, keepdims=True)
        out_i[...] = ref[0:S, :] / n - column * mx
        out_l[...] = ref[S:2 * S, :] / n - column * my


def on_device(T, G, frames, pair_count):
    _, R, F = frames.shape
    S, Q, H, W = F // T, T // 2, LAG // CUTS, F // HALVES
    NB = R // H
    steps = G.bit_length() - 1
    f32, bf16 = jnp.float32, jnp.bfloat16
    V, D = pltpu.VMEM, pltpu.SemaphoreType.DMA
    vmem = pl.BlockSpec(memory_space=pltpu.VMEM)
    own, whole = pl.pallas_call(
        functools.partial(kernel, T, G),
        out_shape=(jax.ShapeDtypeStruct((2 * S + EXTRA, F), f32),) * 2,
        in_specs=[pl.BlockSpec(memory_space=pltpu.SMEM), pl.BlockSpec(memory_space=pl.ANY)],
        out_specs=(vmem,) * 2,
        scratch_shapes=[
            V((NB, H, F), bf16),
            V((NB, F + PAD, H), bf16),
            V((CUTS, H, F), bf16),
            V((CUTS, H, F), bf16),
            V((F + PAD, F), f32),
            V((EXTRA, F), f32),
            V((2, Q, S, F), f32),
            V((HALVES, 2, Q, S + EXTRA, W), f32),
            V((Q, S, F), f32),
            V((HALVES, Q, S + EXTRA, W), f32),
            V((Q - 1, S, F), f32),
            V((HALVES, Q - 1, S + EXTRA, W), f32),
            V((steps + 1, S, F), f32),
            V((HALVES, steps + 1, S + EXTRA, W), f32),
            V((steps, S, F), f32),
            V((HALVES, steps, S + EXTRA, W), f32),
            D((NB,)),
            D((2, CUTS)),
            D((2, CUTS)),
            D((1 + HALVES,)),
            D((1 + HALVES,)),
            D((1 + HALVES, Q - 1)),
            D((1 + HALVES, Q - 1)),
            D((1 + HALVES, steps)),
            D((1 + HALVES, steps)),
        ],
        compiler_params=pltpu.CompilerParams(
            collective_id=0, has_side_effects=True, vmem_limit_bytes=48 * 1024 * 1024
        ),
    )(pair_count, frames)
    return pl.pallas_call(
        centre,
        out_shape=(
            jax.ShapeDtypeStruct((1, S, F), f32),
            jax.ShapeDtypeStruct((1, S, F), f32),
            jax.ShapeDtypeStruct((S, F), f32),
            jax.ShapeDtypeStruct((S, F), f32),
        ),
        in_specs=[vmem, vmem],
        out_specs=(vmem,) * 4,
        compiler_params=pltpu.CompilerParams(vmem_limit_bytes=4 * 1024 * 1024),
    )(own, whole)


def solution(mesh):
    in_specs = (P("group", "tm", None), P("group"))
    out_specs = (P("group", "tm", None), P("group", "tm", None), P("tm", None), P("tm", None))
    body = functools.partial(on_device, mesh.shape["tm"], mesh.shape["group"])
    return jax.shard_map(
        body, mesh=mesh, in_specs=in_specs, out_specs=out_specs, check_vma=False
    )
```

```python
import functools

import jax
import jax.numpy as jnp
from jax import lax
from jax.experimental import pallas as pl
from jax.experimental.pallas import tpu as pltpu
from jax.sharding import PartitionSpec as P

LAG = 2048
MESH = pl.DeviceIdType.MESH
PAD = 16
EXTRA = 8
CUTS = 4
HALVES = 2


def kernel(
    T, G, count_ref, frames_ref, own_ref, all_ref,
    x, xt, head, tail, acc, sx, ai, al, r1i, r1l, r2i, r2l, zi, zl, zri, zrl,
    ld, hs, hr, s1, e1, s2, e2, sz, ez, sf,
):
    F = frames_ref.shape[2]
    R = frames_ref.shape[1]
    H = LAG // CUTS
    NB = R // H
    W = F // HALVES
    S = F // T
    Q = T // 2
    steps = G.bit_length() - 1
    me = lax.axis_index("tm")
    z = lax.axis_index("group")
    c = lax.rem(me, 2)
    q = lax.div(me, 2)
    partner = me + 1 - 2 * c
    count = count_ref[0]

    def remote(src, dst, a, b, dev):
        return pltpu.make_async_remote_copy(
            src_ref=src, dst_ref=dst, send_sem=a, recv_sem=b,
            device_id=dev, device_id_type=MESH,
        )

    def load(i):
        return pltpu.make_async_copy(frames_ref.at[0, pl.ds(i * H, H)], x.at[i], ld.at[i])

    for i in range(NB):
        load(i).start()

    zpeer = []
    for k in range(steps):
        bit = lax.rem(lax.div(z, 2**k), 2)
        zpeer.append(z + 2**k * (1 - 2 * bit))
    relay = G == 4
    if relay:
        inner = lax.div(z + 1, 2) == 1
        outer = z + 2 * lax.div(z, 2) - 1
        zpeer[1] = 3 - z
    barrier = pltpu.get_barrier_semaphore()
    for k in range(1, T):
        pl.semaphore_signal(
            barrier, inc=1, device_id={"tm": lax.rem(me + k, T)}, device_id_type=MESH
        )
    for k in range(steps):
        pl.semaphore_signal(barrier, inc=1, device_id={"group": zpeer[k]}, device_id_type=MESH)
    pl.semaphore_wait(barrier, T - 1 + steps)

    def kept(b):
        if T != 8:
            return CUTS // 2
        turn = lax.rem(b, 2) * (1 - lax.rem(lax.div(b, 2), 2))
        return CUTS // 2 + turn * (2 * lax.div(b, 4) - 1)

    before = lax.rem(me + T - 1, T)

    def send_head(j):
        return remote(
            frames_ref.at[0, pl.ds(j * H, H)], head.at[j], hs.at[0, j], hr.at[0, j], {"tm": me - 1}
        )

    def send_tail(j):
        return remote(
            frames_ref.at[0, pl.ds(R - LAG + j * H, H)], tail.at[j], hs.at[1, j], hr.at[1, j],
            {"tm": me + 1},
        )

    def sent(act):
        for j in range(CUTS):
            @pl.when((me > 0) & (j < kept(before)))
            def _():
                act(send_head(j))

            @pl.when((me < T - 1) & (j >= kept(me)))
            def _():
                act(send_tail(j))

    sent(lambda copy: copy.start())

    def put_transposed(block, base, slot):
        rows = lax.broadcasted_iota(jnp.int32, (H, 128), 0) + base
        keep = jnp.where(rows < count, 1.0, 0.0).astype(jnp.bfloat16)
        masked = block * jnp.concatenate([keep] * (F // 128), axis=1)
        xt[slot, 0:F, :] = masked.T
        cols = lax.broadcasted_iota(jnp.int32, (PAD, H), 1) + base
        xt[slot, F:, :] = jnp.where(cols < count, 1.0, 0.0).astype(jnp.bfloat16)

    def product(slot, block):
        return jnp.dot(xt[slot], block, preferred_element_type=jnp.float32)

    acc[...] = jnp.zeros_like(acc)

    def inst_step(i, carry):
        for j in (2 * i, 2 * i + 1):
            load(j).wait()
            put_transposed(x[j], me * R + j * H, j)
        acc[...] += product(2 * i, x[2 * i]) + product(2 * i + 1, x[2 * i + 1])
        return carry

    lax.fori_loop(0, NB // 2, inst_step, 0)
    for d in range(T):
        ai[d % 2, d // 2] = acc[d * S:(d + 1) * S, :]
    sx[...] = acc[F:F + EXTRA, :]
    p1i = remote(ai.at[1 - c], r1i, s1.at[0], e1.at[0], {"tm": partner})
    p1i.start()

    acc[...] = jnp.zeros_like(acc)

    def lag_step(i, carry):
        j = 2 * i
        acc[...] += product(j, x[j + CUTS]) + product(j + 1, x[j + 1 + CUTS])
        return carry

    lax.fori_loop(0, (NB - CUTS) // 2, lag_step, 0)

    def spread(buf, landed, row):
        out = []
        for k in range(1, Q):
            q2 = lax.rem(q + k, Q)
            out.append(remote(
                buf.at[c, q2], landed.at[k - 1], s2.at[row, k - 1], e2.at[row, k - 1],
                {"tm": 2 * q2 + c},
            ))
        return out

    p1i.wait_recv()
    for k in range(Q):
        ai[c, k] += r1i[k]
    square = Q == 4
    if square:
        side, level = lax.rem(q, 2), lax.div(q, 2)
        across = q + 1 - 2 * side
        over = remote(
            ai.at[c, pl.ds(2 - 2 * level, 2)], r2i.at[pl.ds(0, 2)], s2.at[0, 0], e2.at[0, 0],
            {"tm": 2 * lax.rem(q + 2, Q) + c},
        )
        over.start()
        p2i = [remote(
            ai.at[c, across], r2i.at[2], s2.at[0, 1], e2.at[0, 1], {"tm": 2 * across + c}
        )]
    else:
        p2i = spread(ai, r2i, 0)

    def heads():
        def head_step(j, carry):
            send_head(j).wait_recv()
            acc[...] += product(NB - CUTS + j, head[j])
            return carry

        lax.fori_loop(0, kept(me), head_step, 0)

    def tails():
        def tail_step(j, carry):
            send_tail(j).wait_recv()
            put_transposed(tail[j], me * R - LAG + j * H, j)
            acc[...] += product(j, x[j])
            return carry

        lax.fori_loop(kept(before), CUTS, tail_step, 0)

    pl.when((me < T - 1) & (c == 0))(heads)
    pl.when(me > 0)(tails)
    pl.when((me < T - 1) & (c == 1))(heads)

    which = lax.broadcasted_iota(jnp.int32, (EXTRA, W), 0)
    p1l = []
    for h in range(HALVES):
        cols = slice(h * W, (h + 1) * W)
        sums = jnp.where(which < 3, sx[:, cols], acc[F:F + EXTRA, cols])
        for d in range(T):
            al[h, d % 2, d // 2, 0:S, :] = acc[d * S:(d + 1) * S, cols]
            al[h, d % 2, d // 2, S:, :] = sums
        p1l.append(remote(al.at[h, 1 - c], r1l.at[h], s1.at[1 + h], e1.at[1 + h], {"tm": partner}))
        p1l[h].start()

    if square:
        over.wait_recv()
        for k in range(2):
            ai[c, 2 * level + k] += r2i[k]
    for copy in p2i:
        copy.start()

    class Far:
        def __init__(self, buf, landed, row):
            self.swap = remote(
                buf.at[1], landed.at[1], sz.at[row, 1], ez.at[row, 1], {"group": zpeer[1]}
            )
            self.onward = remote(
                landed.at[1], landed.at[1], sf.at[row], ez.at[row, 1], {"group": outer}
            )

        def start(self):
            @pl.when(inner)
            def _():
                self.swap.start()

        def wait_recv(self):
            self.swap.wait_recv()

            @pl.when(inner)
            def _():
                self.onward.start()

        def wait_send(self):
            @pl.when(inner)
            def _():
                self.swap.wait_send()
                self.onward.wait_send()

    def exchange(buf, landed, k, row):
        if relay and k == 1:
            return Far(buf, landed, row)
        return remote(
            buf.at[k], landed.at[k], sz.at[row, k], ez.at[row, k], {"group": zpeer[k]}
        )

    p2l = []
    for h in range(HALVES):
        p1l[h].wait_recv()
        for k in range(Q):
            al[h, c, k] += r1l[h, k]
        p2l.append(spread(al.at[h], r2l.at[h], 1 + h))
        for copy in p2l[h]:
            copy.start()

    for copy in p2i:
        copy.wait_recv()
    total = ai[c, q]
    for k in range(2 if square else 0, Q - 1):
        total = total + r2i[k]
    zi[0] = total
    zi_copies = [exchange(zi, zri, k, 0) for k in range(steps)]
    zl_copies = [
        [exchange(zl.at[h], zrl.at[h], k, 1 + h) for k in range(steps)] for h in range(HALVES)
    ]
    zi_copies[0].start()

    def advance(copies, buf, landed, k):
        copies[k].wait_recv()
        buf[k + 1] = buf[k] + landed[k]
        if k + 1 < steps:
            copies[k + 1].start()

    for k in range(steps - 1):
        advance(zi_copies, zi, zri, k)

    number = count.astype(jnp.float32)
    for h in range(HALVES):
        for copy in p2l[h]:
            copy.wait_recv()
        total = al[h, c, q]
        for k in range(Q - 1):
            total = total + r2l[h, k]
        zl[h, 0, 0:S, :] = total[0:S]
        zl[h, 0, S:, :] = jnp.where(which < 6, total[S:], number)
        zl_copies[h][0].start()

    def out(ref, k):
        ref[0:S, :] = zi[k]
        for h in range(HALVES):
            ref[S:, h * W:(h + 1) * W] = zl[h, k]

    out(own_ref, 0)
    advance(zi_copies, zi, zri, steps - 1)
    for k in range(steps):
        for h in range(HALVES):
            advance(zl_copies[h], zl.at[h], zrl.at[h], k)
    out(all_ref, steps)

    sent(lambda copy: copy.wait_send())
    if square:
        over.wait_send()
    for group in [[p1i], p1l, p2i, *p2l, zi_copies, *zl_copies]:
        for copy in group:
            copy.wait_send()


def centre(own_ref, all_ref, gi_ref, gl_ref, pi_ref, po_ref):
    S, F = pi_ref.shape
    rows = lax.broadcasted_iota(jnp.int32, (S, F), 0) + lax.axis_index("tm") * S
    cols = lax.broadcasted_iota(jnp.int32, (S, F), 1)
    for ref, out_i, out_l in ((own_ref, gi_ref.at[0], gl_ref.at[0]), (all_ref, pi_ref, po_ref)):
        n = ref[2 * S + 6:2 * S + 7, :]
        mx = ref[2 * S:2 * S + 1, :] / n
        my = ref[2 * S + 3:2 * S + 4, :] / n
        wide = jnp.where(rows == cols, jnp.broadcast_to(mx, (S, F)), 0.0)
        column = jnp.sum(wide, axis=1, keepdims=True)
        out_i[...] = ref[0:S, :] / n - column * mx
        out_l[...] = ref[S:2 * S, :] / n - column * my


def on_device(T, G, frames, pair_count):
    _, R, F = frames.shape
    S, Q, H, W = F // T, T // 2, LAG // CUTS, F // HALVES
    NB = R // H
    steps = G.bit_length() - 1
    f32, bf16 = jnp.float32, jnp.bfloat16
    V, D = pltpu.VMEM, pltpu.SemaphoreType.DMA
    vmem = pl.BlockSpec(memory_space=pltpu.VMEM)
    own, whole = pl.pallas_call(
        functools.partial(kernel, T, G),
        out_shape=(jax.ShapeDtypeStruct((2 * S + EXTRA, F), f32),) * 2,
        in_specs=[pl.BlockSpec(memory_space=pltpu.SMEM), pl.BlockSpec(memory_space=pl.ANY)],
        out_specs=(vmem,) * 2,
        scratch_shapes=[
            V((NB, H, F), bf16),
            V((NB, F + PAD, H), bf16),
            V((CUTS, H, F), bf16),
            V((CUTS, H, F), bf16),
            V((F + PAD, F), f32),
            V((EXTRA, F), f32),
            V((2, Q, S, F), f32),
            V((HALVES, 2, Q, S + EXTRA, W), f32),
            V((Q, S, F), f32),
            V((HALVES, Q, S + EXTRA, W), f32),
            V((Q - 1, S, F), f32),
            V((HALVES, Q - 1, S + EXTRA, W), f32),
            V((steps + 1, S, F), f32),
            V((HALVES, steps + 1, S + EXTRA, W), f32),
            V((steps, S, F), f32),
            V((HALVES, steps, S + EXTRA, W), f32),
            D((NB,)),
            D((2, CUTS)),
            D((2, CUTS)),
            D((1 + HALVES,)),
            D((1 + HALVES,)),
            D((1 + HALVES, Q - 1)),
            D((1 + HALVES, Q - 1)),
            D((1 + HALVES, steps)),
            D((1 + HALVES, steps)),
            D((1 + HALVES,)),
        ],
        compiler_params=pltpu.CompilerParams(
            collective_id=0, has_side_effects=True, vmem_limit_bytes=48 * 1024 * 1024
        ),
    )(pair_count, frames)
    return pl.pallas_call(
        centre,
        out_shape=(
            jax.ShapeDtypeStruct((1, S, F), f32),
            jax.ShapeDtypeStruct((1, S, F), f32),
            jax.ShapeDtypeStruct((S, F), f32),
            jax.ShapeDtypeStruct((S, F), f32),
        ),
        in_specs=[vmem, vmem],
        out_specs=(vmem,) * 4,
        compiler_params=pltpu.CompilerParams(vmem_limit_bytes=4 * 1024 * 1024),
    )(own, whole)


def solution(mesh):
    in_specs = (P("group", "tm", None), P("group"))
    out_specs = (P("group", "tm", None), P("group", "tm", None), P("tm", None), P("tm", None))
    body = functools.partial(on_device, mesh.shape["tm"], mesh.shape["group"])
    return jax.shard_map(
        body, mesh=mesh, in_specs=in_specs, out_specs=out_specs, check_vma=False
    )
```
